32 devices in a mesh: groups: 2 (over y), blk: 4 (over z), occ: 2 (over x), rep: 2 (over core).
Axes of the slice: x: 2, y: 2, z: 4, core: 2. Of those that a mesh axis runs over, the one named last changes fastest.
Arguments:
- amplitudes: float32 [1536, 4, 256], P(('groups', 'occ'), 'blk', 'rep'), parts along dimension 0, may hold values from -6 to 6
- integrals: float32 [4096, 4, 256], P(('groups', 'blk'), None, 'rep'), parts along dimension 0, may hold values from -0.0625 to 0.0625, as said below
Outputs:
- symmetrized: float32 [1536, 2048], P(('groups', 'occ'), ('blk', 'rep')), parts along dimension 0
The draws below stay inside these ranges and needn't reach their ends.
There are 2 independent parts, one for each index of `groups`. The reference program is written for one: setup_inputs(seed, part) draws one part's arguments, and reference() takes and returns one part's arrays. A program takes and returns all parts, laid end to end along the dimension named above; each array names one. Nothing has to cross between parts.
Inputs may be any that keep to these rules, and one draw needn't show every extreme that they name: integrals[2047 - a, 3 - c, 255 - w] equals integrals[a, c, w]: pairs are listed so that a pair's transpose stands at the mirrored position.
All inputs are finite; a program needn't handle non-finite values.
Results may differ from the reference program's by a relative error of at most 0.00007.
Values sent between devices are 32-bit elements; how exact they have to be, the bound alone decides.
No kernel may reach another device: no remote copies, remote signals or barrier semaphores. Data moves between devices by JAX's collectives and lax.ppermute only.
A program may use at most 64 MiB of HBM per device.

```python
import jax
import jax.numpy as jnp
from jax import lax

CD_BLK = 256
SPANS = 4
NIJ = 768
NAB = 2048


def draw_integrals(key, part):
    extent = (NAB, SPANS, CD_BLK)
    sample = jnp.clip(jax.random.normal(key, extent, jnp.float32), -4.0, 4.0)
    paired = jnp.clip((sample + sample[::-1, ::-1, ::-1]) * 0.5 ** 0.5, -2.0, 2.0)
    return paired / jnp.sqrt(jnp.float32(SPANS * CD_BLK))


def steps_of(stream_key, shape, split, least, top_value):
    level = 1.0
    for dim, blocks in split:
        draws = jax.random.uniform(jax.random.fold_in(jax.random.fold_in(stream_key, 6), dim), (blocks,), jnp.float32, least / len(split), top_value / len(split))
        level = level * jnp.repeat(jnp.exp(draws), shape[dim] // blocks).reshape((-1,) + (1,) * (len(shape) - 1 - dim))
    return level


def bell_draw(stream_key, shape, scale, reach, shards=(), held_as=jnp.bfloat16):
    entries = jax.random.normal(stream_key, shape, jnp.float32) * scale
    if len(shards) > 0:
        entries = steps_of(stream_key, shape, shards, -0.22, 0.18) * entries
    return jnp.clip(entries, min=-reach, max=reach).astype(held_as)


def setup_inputs(seed: int = 0, part: int = 0) -> dict:
    key_list = jax.random.split(jax.random.key(seed), 3)
    own_keys = jax.random.split(jax.random.fold_in(key_list[2], part), 3)
    amplitudes = bell_draw(own_keys[0], (NIJ, SPANS, CD_BLK), 1.0, 6.0, ((0, 2), (1, 4), (2, 2)), jnp.float32)
    integrals = draw_integrals(jax.random.fold_in(jax.random.fold_in(key_list[2], part), 71), part)
    return {"amplitudes": amplitudes, "integrals": integrals}


def reference(amplitudes, integrals):
    left_rows = amplitudes.reshape(amplitudes.shape[0], -1)
    right_rows = integrals.reshape(integrals.shape[0], -1)
    ladder = lax.dot_general(left_rows, right_rows, (((1,), (1,)), ((), ())), precision=lax.Precision.HIGHEST, preferred_element_type=jnp.float32)
    return ladder + ladder[::-1, ::-1]
```

```python
import jax
import jax.numpy as jnp
from jax import lax
from jax.sharding import PartitionSpec as P

PLANE = ("blk", "occ", "rep")


def mirrored(array):
    size = lax.axis_size(PLANE)
    return lax.ppermute(array, PLANE, [(i, size - 1 - i) for i in range(size)])


def shifted(array, offset, flip):
    blks, occs, reps = (lax.axis_size(name) for name in PLANE)
    half = blks // 2
    pairs = []
    for blk in range(blks):
        target_blk = blk // half * half + (blk % half + offset) % half
        for occ in range(occs):
            for rep in range(reps):
                target = (target_blk, occs - 1 - occ, reps - 1 - rep) if flip else (target_blk, occ, rep)
                source_index = (blk * occs + occ) * reps + rep
                target_index = (target[0] * occs + target[1]) * reps + target[2]
                pairs.append((source_index, target_index))
    return lax.ppermute(array, PLANE, pairs)


def product(rows, columns):
    return lax.dot_general(
        rows,
        columns,
        (((1,), (1,)), ((), ())),
        precision=lax.Precision.HIGHEST,
        preferred_element_type=jnp.float32,
    )


def shards(amplitudes, integrals):
    blks, _, reps = (lax.axis_size(name) for name in PLANE)
    half = blks // 2
    blk = lax.axis_index("blk")
    rep = lax.axis_index("rep")
    width = integrals.shape[0] // reps
    depth = integrals.shape[2]

    own = amplitudes[:, 0, :]
    transposed = mirrored(own)
    summed = own + transposed[::-1, ::-1]
    summed_back = own[::-1, ::-1] + transposed

    def columns_of(position, owner):
        return lax.dynamic_slice(integrals, (owner * width, position, 0), (width, 1, depth))[:, 0, :]

    terms = []
    for offset in range(half):
        position = blk // half * half + (blk % half - offset) % half
        near = summed if offset == 0 else shifted(summed, offset, False)
        terms.append((near, position))
        terms.append((shifted(summed_back, offset, True), blks - 1 - position))
    others = sum(product(rows, columns_of(position, 1 - rep)) for rows, position in terms)
    mine = sum(product(rows, columns_of(position, rep)) for rows, position in terms)
    return mine + lax.ppermute(others, "rep", [(0, 1), (1, 0)])


def solution(mesh):
    return jax.shard_map(
        shards,
        mesh=mesh,
        in_specs=(P(("groups", "occ"), "blk", "rep"), P(("groups", "blk"), None, "rep")),
        out_specs=P(("groups", "occ"), ("blk", "rep")),
        check_vma=False,
    )
```
